32 devices in a mesh: clips: 2 (over y), tiles: 16 (over z, x, core).
Axes of the slice: x: 2, y: 2, z: 4, core: 2. Of those that a mesh axis runs over, the one named last changes fastest.
Arguments:
- frames: bfloat16 [4, 64, 256, 128], P(None, None, ('clips', 'tiles')), parts along dimension 2, may hold values from -6 to 6
- motion_forward: int32 [3, 512], P(None, ('clips', 'tiles')), parts along dimension 1, may hold values from 0 to 255, as said below
- motion_backward: int32 [3, 512], P(None, ('clips', 'tiles')), parts along dimension 1, may hold values from 0 to 255, as said below
- join_weight: bfloat16 [2, 64, 128], replicated, may hold values from -0.5 to 0.5
- conv_weight: bfloat16 [2, 4, 9, 64, 64], replicated, may hold values from -0.125 to 0.125
Outputs:
- forward_features: bfloat16 [4, 64, 256, 128], P(None, None, ('clips', 'tiles')), parts along dimension 2
- backward_features: bfloat16 [4, 64, 256, 128], P(None, None, ('clips', 'tiles')), parts along dimension 2
The draws below stay inside these ranges and needn't reach their ends.
There are 2 independent parts, one for each index of `clips`. The reference program is written for one: setup_inputs(seed, part) draws one part's arguments, and reference() takes and returns one part's arrays. A program takes and returns all parts, laid end to end along the dimension named above; an argument that names none is the same for every part. Nothing has to cross between parts.
Inputs may be any that keep to these rules, and one draw needn't show every extreme that they name: `motion_forward`: entries are block numbers of the frame; block number k lies in rows held by device k // 16. A block of device d takes a block of a device at most 2 away from d, at most two block columns to either side of its own column. Of the 16 blocks of one device, either none or exactly 4 take blocks of any one other device; in every frame some device takes 4 blocks from each device up to 2 away on both sides. `motion_backward`: entries are block numbers of the frame; block number k lies in rows held by device k // 16. A block of device d takes a block of a device at most 2 away from d, at most two block columns to either side of its own column. Of the 16 blocks of one device, either none or exactly 4 take blocks of any one other device; in every frame some device takes 4 blocks from each device up to 2 away on both sides.
All inputs are finite; a program needn't handle non-finite values.
Results may differ from the reference program's by a relative error of at most 0.018.
Values may be sent and summed in bfloat16 or wider, within the bound.
A program may use at most 64 MiB of HBM per device.

```python
import jax
import jax.numpy as jnp
from jax import lax

C = 64
ROWS_DEV = 8
COLS = 128
FRAMES = 4
CONVS = 4
BS = 8
REACH = 2
HEIGHT = 128
N_TILES = 16


def motion_lists(key, salt):
    block_count = ROWS_DEV // BS * (COLS // BS)
    capacity = block_count // (2 * REACH)
    block_rows = ROWS_DEV // BS
    block_cols = COLS // BS
    band_width = N_TILES // 8
    offset_table = jnp.array([offset for offset in range(-REACH, REACH + 1) if offset != 0], jnp.int32)
    frame_keys = jax.random.split(jax.random.fold_in(key, salt), FRAMES - 1)

    def one_frame(frame_key):
        center = jax.random.randint(jax.random.fold_in(frame_key, 1), (), 0, N_TILES)

        def one_device(device):
            device_key = jax.random.fold_in(frame_key, device + 7)
            fast_strip = jnp.abs(device - center) <= band_width
            slot_offset = jnp.repeat(offset_table, capacity)
            allowed = fast_strip | (jnp.abs(slot_offset) == 1)
            source_strip = device + slot_offset
            usable = allowed & (source_strip >= 0) & (source_strip < N_TILES)
            slot_offset = jnp.where(usable, slot_offset, 0)
            mixing = jax.random.permutation(jax.random.fold_in(device_key, 2), block_count)
            dest_offset = slot_offset[mixing]
            positions = jnp.arange(block_count).astype(jnp.int32)
            dest_col = positions % block_cols
            source_row = jax.random.randint(jax.random.fold_in(device_key, 3), (block_count,), 0, block_rows)
            drift = jax.random.randint(jax.random.fold_in(device_key, 4), (block_count,), -2, 3)
            source_col = jnp.clip(dest_col + drift, 0, block_cols - 1)
            return ((device + dest_offset) * block_count + source_row * block_cols + source_col).astype(jnp.int32)
        return jax.vmap(one_device)(jnp.arange(N_TILES).astype(jnp.int32)).reshape(-1)
    return jax.vmap(one_frame)(frame_keys)


def draw_motion_forward(key, part):
    return motion_lists(key, 11)


def draw_motion_backward(key, part):
    return motion_lists(key, 23)


def levels(rng, extent, cuts, smallest, high):
    def one(dim, shards_of):
        draws = jax.random.uniform(jax.random.fold_in(jax.random.fold_in(rng, 6), dim), (shards_of,), jnp.float32, smallest / len(cuts), high / len(cuts))
        return jnp.repeat(jnp.exp(draws), extent[dim] // shards_of).reshape((-1,) + (1,) * (len(extent) - dim - 1))

    factor_of = one(*cuts[0])
    for cut in cuts[1:]:
        factor_of = factor_of * one(*cut)
    return factor_of


def normal_values(stream_key, extent, width, limit, pieces=(), dtype=jnp.bfloat16):
    drawn = jax.random.normal(stream_key, extent, jnp.float32) * width
    if len(pieces) > 0:
        drawn = levels(stream_key, extent, pieces, -0.22, 0.18) * drawn
    return jnp.clip(drawn, min=-limit, max=limit).astype(dtype)


def setup_inputs(seed: int = 0, part: int = 0) -> dict:
    key_list = jax.random.split(jax.random.key(seed), 6)
    part_splits = jax.random.split(jax.random.fold_in(key_list[5], part), 6)
    frames = normal_values(part_splits[0], (FRAMES, C, HEIGHT, COLS), 1.0, 6.0, ((2, 16),))
    motion_forward = draw_motion_forward(jax.random.fold_in(jax.random.fold_in(key_list[5], part), 71), part)
    motion_backward = draw_motion_backward(jax.random.fold_in(jax.random.fold_in(key_list[5], part), 71), part)
    join_weight = normal_values(key_list[3], (2, C, 2 * C), (2 * C) ** -0.5, 0.5)
    conv_weight = normal_values(key_list[4], (2, CONVS, 9, C, C), (36 * C) ** -0.5, 0.125)
    return {"frames": frames, "motion_forward": motion_forward, "motion_backward": motion_backward, "join_weight": join_weight, "conv_weight": conv_weight}


def frame_blocks(field):
    channels, height, breadth = field.shape
    block_grid = field.reshape(channels, height // BS, BS, breadth // BS, BS)
    return block_grid.transpose(1, 3, 0, 2, 4).reshape(-1, channels * BS * BS)


def blocks_frame(blocks, channels, height, breadth):
    block_grid = blocks.reshape(height // BS, breadth // BS, channels, BS, BS)
    return block_grid.transpose(2, 0, 3, 1, 4).reshape(channels, height, breadth)


def refine(aligned, inputs, join_matrix, conv_layers):
    channels, height, breadth = inputs.shape
    mixed = jnp.einsum("oc,chw->ohw", join_matrix[:, :channels].astype(jnp.float32), aligned.astype(jnp.float32))
    mixed = mixed + jnp.einsum("oc,chw->ohw", join_matrix[:, channels:].astype(jnp.float32), inputs.astype(jnp.float32))
    carried = lax.optimization_barrier(mixed.astype(jnp.bfloat16))
    for layer_index in range(conv_layers.shape[0]):
        widened = carried.astype(jnp.float32)
        active = jnp.where(widened >= 0, widened, 0.1 * widened).astype(jnp.bfloat16)
        active = lax.optimization_barrier(active)
        padded = jnp.pad(active, ((0, 0), (1, 1), (1, 1))).astype(jnp.float32)
        summed = jnp.zeros(widened.shape, jnp.float32)
        for tap_index in range(9):
            row_shift = tap_index // 3
            column_shift = tap_index % 3
            window = padded[:, row_shift:row_shift + height, column_shift:column_shift + breadth]
            kernel = conv_layers[layer_index, tap_index].astype(jnp.float32)
            summed = summed + jnp.einsum("oi,ihw->ohw", kernel, window)
        carried = lax.optimization_barrier((widened + summed).astype(jnp.bfloat16))
    return carried


def reference(frames, motion_forward, motion_backward, join_weight, conv_weight):
    frame_total, channels, height, breadth = frames.shape
    forward = []
    carried = None
    for frame_time in range(frame_total):
        if frame_time == 0:
            aligned = jnp.zeros(frames.shape[1:], jnp.bfloat16)
        else:
            moved = jnp.take(frame_blocks(carried), motion_forward[frame_time - 1].astype(jnp.int32), axis=0)
            aligned = blocks_frame(moved, channels, height, breadth)
        carried = refine(aligned, frames[frame_time], join_weight[0], conv_weight[0])
        forward.append(carried)
    backward = []
    carried = None
    for frame_time in range(frame_total - 1, -1, -1):
        if frame_time == frame_total - 1:
            aligned = jnp.zeros(frames.shape[1:], jnp.bfloat16)
        else:
            moved = jnp.take(frame_blocks(carried), motion_backward[frame_time].astype(jnp.int32), axis=0)
            aligned = blocks_frame(moved, channels, height, breadth)
        carried = refine(aligned, frames[frame_time], join_weight[1], conv_weight[1])
        backward.append(carried)
    return jnp.stack(forward), jnp.stack(backward[::-1])
```

```python
import functools

import jax
import jax.numpy as jnp
from jax import lax
from jax.experimental import pallas as pl
from jax.experimental.pallas import tpu as pltpu
from jax.sharding import PartitionSpec as P

BS = 8
REACH = 2
OFFSETS = tuple(o for o in range(-REACH, REACH + 1) if o != 0)


def leaky(value):
    return jnp.where(value >= 0, value, 0.1 * value)


def sweep_kernel(
    dims,
    x_ref,
    mf_ref,
    mb_ref,
    wj_ref,
    wc_ref,
    out_ref,
    mine,
    theirs,
    table_v,
    table_s,
    cand,
    packed,
    landed,
    aligned,
    h_ref,
    z_ref,
    edge_out,
    edge_in,
    m_send,
    m_recv,
    f_send,
    f_recv,
    e_send,
    e_recv,
    t_sem,
):
    frame_count, rows, cols, channels, layers, devices = dims
    lanes = 2 * channels
    bcols = cols // BS
    bc = rows // BS * bcols
    cap = bc // (2 * REACH)
    cell = BS * BS
    own = rows * cols
    halo = layers * cols
    me = lax.axis_index("tiles")

    def present(offset):
        return (me + offset >= 0) & (me + offset < devices)

    def motion_copy(oi):
        return pltpu.make_async_remote_copy(
            src_ref=mine,
            dst_ref=theirs.at[len(OFFSETS) - 1 - oi],
            send_sem=m_send.at[oi],
            recv_sem=m_recv.at[len(OFFSETS) - 1 - oi],
            device_id={"tiles": me + OFFSETS[oi]},
            device_id_type=pl.DeviceIdType.MESH,
        )

    def motion_arrival(oi):
        return pltpu.make_async_remote_copy(
            src_ref=mine,
            dst_ref=theirs.at[oi],
            send_sem=m_send.at[oi],
            recv_sem=m_recv.at[oi],
            device_id={"tiles": me + OFFSETS[oi]},
            device_id_type=pl.DeviceIdType.MESH,
        )

    def feature_copy(step, oi, slot):
        return pltpu.make_async_remote_copy(
            src_ref=packed.at[step, oi],
            dst_ref=landed.at[step, slot],
            send_sem=f_send.at[step, oi],
            recv_sem=f_recv.at[step, slot],
            device_id={"tiles": me + OFFSETS[oi]},
            device_id_type=pl.DeviceIdType.MESH,
        )

    def edge_copy(step, side, slot):
        return pltpu.make_async_remote_copy(
            src_ref=edge_out.at[step, side],
            dst_ref=edge_in.at[step, slot],
            send_sem=e_send.at[step, side],
            recv_sem=e_recv.at[step, slot],
            device_id={"tiles": me + (1 if side else -1)},
            device_id_type=pl.DeviceIdType.MESH,
        )

    barrier = pltpu.get_barrier_semaphore()
    for offset in OFFSETS:
        @pl.when(present(offset))
        def _():
            pl.semaphore_signal(
                barrier, inc=1, device_id={"tiles": me + offset},
                device_id_type=pl.DeviceIdType.MESH,
            )

    mine[...] = jnp.zeros(mine.shape, jnp.int32)
    for step in range(frame_count - 1):
        mine[step:step + 1, 0:bc] = mf_ref[step:step + 1, :]
        back = frame_count - 2 - step
        mine[frame_count - 1 + step:frame_count + step, 0:bc] = mb_ref[back:back + 1, :]

    peers = jnp.minimum(me, REACH) + jnp.minimum(devices - 1 - me, REACH)
    pl.semaphore_wait(barrier, peers)

    for oi, offset in enumerate(OFFSETS):
        @pl.when(present(offset))
        def _():
            motion_copy(oi).start()

    lane = lax.broadcasted_iota(jnp.int32, mine.shape, 1)

    def prefix(flags):
        total = flags
        shift = 1
        while shift < bc:
            total = total + jnp.where(lane >= shift, pltpu.roll(total, shift, axis=1), 0)
            shift *= 2
        return total - flags

    def owned(motion, device):
        low = device * bc
        return (motion >= low) & (motion < low + bc) & (lane < bc)

    def build_tables():
        motion = mine[...]
        picks = jnp.where(owned(motion, me), motion - me * bc, 0)
        for oi, offset in enumerate(OFFSETS):
            match = owned(motion, me + offset)
            rank = prefix(match.astype(jnp.int32))
            picks = picks + jnp.where(match, bc + cap * oi + jnp.minimum(rank, cap - 1), 0)
        table_v[len(OFFSETS)] = picks
        for oi, offset in enumerate(OFFSETS):
            @pl.when(present(offset))
            def _():
                motion_copy(oi).wait_send()
                motion_arrival(oi).wait_recv()
                wanted = theirs[oi]
                match = owned(wanted, me)
                rank = prefix(match.astype(jnp.int32))
                gathered = jnp.zeros(mine.shape, jnp.int32)
                for slot in range(cap):
                    value = jnp.where(match & (rank == slot), wanted - me * bc, 0)
                    shift = 1
                    while shift < bc:
                        value = value + pltpu.roll(value, shift, axis=1)
                        shift *= 2
                    value = pltpu.roll(value, 1 + slot, axis=1)
                    gathered = jnp.where(lane == bc + slot, value, gathered)
                table_v[oi] = gathered

            @pl.when(jnp.logical_not(present(offset)))
            def _():
                table_v[oi] = jnp.zeros(mine.shape, jnp.int32)
        load = pltpu.make_async_copy(table_v, table_s, t_sem)
        load.start()
        load.wait()

    half = lax.broadcasted_iota(jnp.int32, (rows, BS, lanes), 2) < channels

    def frame_step(t, carry):
        @pl.when(t == 0)
        def _():
            aligned[...] = jnp.zeros(aligned.shape, aligned.dtype)

        @pl.when(t > 0)
        def _():
            step = t - 1
            for oi, offset in enumerate(OFFSETS):
                @pl.when(present(offset))
                def _():
                    for slot in range(cap):
                        ahead = table_s[oi, step, bc + slot]
                        behind = table_s[oi, frame_count - 1 + step, bc + slot]
                        block = jnp.where(half, cand[ahead], cand[behind])
                        packed[step, oi, slot * cell:(slot + 1) * cell, :] = block.reshape(
                            cell, lanes
                        ).astype(jnp.bfloat16)
                    feature_copy(step, oi, len(OFFSETS) - 1 - oi).start()
            for oi, offset in enumerate(OFFSETS):
                @pl.when(present(offset))
                def _():
                    feature_copy(step, oi, oi).wait_recv()
                    cand[bc + cap * oi:bc + cap * (oi + 1)] = (
                        landed[step, oi].astype(jnp.float32).reshape(cap, BS, BS, lanes)
                    )
            for j in range(bc):
                ahead = table_s[len(OFFSETS), step, j]
                behind = table_s[len(OFFSETS), frame_count - 1 + step, j]
                aligned[:, j * BS:(j + 1) * BS, :] = jnp.where(half, cand[ahead], cand[behind])

        both = jnp.concatenate(
            [aligned[...].reshape(own, lanes).astype(jnp.bfloat16), x_ref[t]], axis=1
        )
        first = jnp.dot(both, wj_ref[...], preferred_element_type=jnp.float32).astype(jnp.bfloat16)
        h_ref[halo:halo + own, :] = first
        edge_out[t, 0] = first[:halo]
        edge_out[t, 1] = first[own - halo:]
        for side in range(2):
            @pl.when(present(1 if side else -1))
            def _():
                edge_copy(t, side, 1 - side).start()
        z_ref[0, halo:halo + own, :] = leaky(first.astype(jnp.float32)).astype(jnp.bfloat16)

        @pl.when(t == 0)
        def _():
            build_tables()

        for side in range(2):
            start = side * (halo + own)

            @pl.when(present(1 if side else -1))
            def _():
                edge_copy(t, side, side).wait_recv()
                edge = edge_in[t, side]
                h_ref[start:start + halo, :] = edge
                z_ref[0, start:start + halo, :] = leaky(edge.astype(jnp.float32)).astype(jnp.bfloat16)

            @pl.when(jnp.logical_not(present(1 if side else -1)))
            def _():
                h_ref[start:start + halo, :] = jnp.zeros((halo, lanes), jnp.bfloat16)
                z_ref[0, start:start + halo, :] = jnp.zeros((halo, lanes), jnp.bfloat16)

        for layer in range(layers):
            out_rows = rows + 2 * (layers - 1 - layer)
            size = out_rows * cols
            source = z_ref.at[layer % 2]
            target = z_ref.at[1 - layer % 2]
            stack = jnp.concatenate(
                [source[(layer + k) * cols:(layer + k) * cols + size, :] for k in range(3)], axis=1
            )
            summed = jnp.dot(stack, wc_ref[layer], preferred_element_type=jnp.float32)
            place = lax.broadcasted_iota(jnp.int32, (size, lanes), 0) % cols
            left = pltpu.roll(summed[:, :lanes], 1, axis=0)
            right = pltpu.roll(summed[:, 2 * lanes:], size - 1, axis=0)
            base = (layer + 1) * cols
            total = h_ref[base:base + size, :].astype(jnp.float32) + summed[:, lanes:2 * lanes]
            total = total + jnp.where(place == 0, 0.0, left)
            total = total + jnp.where(place == cols - 1, 0.0, right)
            rounded = total.astype(jnp.bfloat16)
            if layer < layers - 1:
                h_ref[base:base + size, :] = rounded
                target[base:base + size, :] = leaky(rounded.astype(jnp.float32)).astype(jnp.bfloat16)
                outside = halo - base

                @pl.when(me == 0)
                def _():
                    target[base:halo, :] = jnp.zeros((outside, lanes), jnp.bfloat16)

                @pl.when(me == devices - 1)
                def _():
                    target[halo + own:halo + own + outside, :] = jnp.zeros(
                        (outside, lanes), jnp.bfloat16
                    )
            else:
                out_ref[t] = rounded
                grid = rounded.astype(jnp.float32).reshape(rows, bcols, BS, lanes)
                for j in range(bcols):
                    cand[j] = grid[:, j]
        return carry

    lax.fori_loop(0, frame_count, frame_step, 0)

    for step in range(frame_count):
        for side in range(2):
            @pl.when(present(1 if side else -1))
            def _():
                edge_copy(step, side, side).wait_send()
        if step < frame_count - 1:
            for oi, offset in enumerate(OFFSETS):
                @pl.when(present(offset))
                def _():
                    feature_copy(step, oi, oi).wait_send()


def on_device(frames, motion_forward, motion_backward, join_weight, conv_weight):
    frame_count, channels, rows, cols = frames.shape
    layers = conv_weight.shape[1]
    devices = lax.axis_size("tiles")
    lanes = 2 * channels
    own = rows * cols
    halo = layers * cols
    bc = rows // BS * (cols // BS)
    cap = bc // (2 * REACH)
    sides = len(OFFSETS)
    steps = frame_count - 1

    moved = frames.transpose(0, 2, 3, 1).reshape(frame_count, own, channels)
    x = jnp.concatenate([moved, moved[::-1]], axis=2)
    same = jnp.eye(2, dtype=jnp.bfloat16)
    joined = join_weight.reshape(2, channels, 2, channels).transpose(2, 0, 3, 1)
    wj = (joined[:, :, :, None, :] * same[None, :, None, :, None]).reshape(2 * lanes, lanes)
    taps = conv_weight.reshape(2, layers, 3, 3, channels, channels).transpose(1, 2, 0, 5, 3, 4)
    wc = (taps[:, :, :, :, :, None, :] * same[None, None, :, None, None, :, None]).reshape(
        layers, 3 * lanes, 3 * lanes
    )

    dims = (frame_count, rows, cols, channels, layers, devices)
    vmem = pl.BlockSpec(memory_space=pltpu.VMEM)
    out = pl.pallas_call(
        functools.partial(sweep_kernel, dims),
        out_shape=jax.ShapeDtypeStruct((frame_count, own, lanes), jnp.bfloat16),
        in_specs=[vmem] * 5,
        out_specs=vmem,
        scratch_shapes=[
            pltpu.VMEM((8, 128), jnp.int32),
            pltpu.VMEM((sides, 8, 128), jnp.int32),
            pltpu.VMEM((sides + 1, 8, 128), jnp.int32),
            pltpu.SMEM((sides + 1, 8, 128), jnp.int32),
            pltpu.VMEM((bc + sides * cap, BS, BS, lanes), jnp.float32),
            pltpu.VMEM((steps, sides, cap * BS * BS, lanes), jnp.bfloat16),
            pltpu.VMEM((steps, sides, cap * BS * BS, lanes), jnp.bfloat16),
            pltpu.VMEM((rows, cols, lanes), jnp.float32),
            pltpu.VMEM((own + 2 * halo, lanes), jnp.bfloat16),
            pltpu.VMEM((2, own + 2 * halo, lanes), jnp.bfloat16),
            pltpu.VMEM((frame_count, 2, halo, lanes), jnp.bfloat16),
            pltpu.VMEM((frame_count, 2, halo, lanes), jnp.bfloat16),
            pltpu.SemaphoreType.DMA((sides,)),
            pltpu.SemaphoreType.DMA((sides,)),
            pltpu.SemaphoreType.DMA((steps, sides)),
            pltpu.SemaphoreType.DMA((steps, sides)),
            pltpu.SemaphoreType.DMA((frame_count, 2)),
            pltpu.SemaphoreType.DMA((frame_count, 2)),
            pltpu.SemaphoreType.DMA,
        ],
        compiler_params=pltpu.CompilerParams(
            collective_id=0, has_side_effects=True, vmem_limit_bytes=56 * 1024 * 1024
        ),
    )(x, motion_forward, motion_backward, wj, wc)
    out = out.reshape(frame_count, rows, cols, 2, channels)
    forward = out[:, :, :, 0].transpose(0, 3, 1, 2)
    backward = out[::-1, :, :, 1].transpose(0, 3, 1, 2)
    return forward, backward


def solution(mesh):
    return jax.shard_map(
        on_device,
        mesh=mesh,
        in_specs=(
            P(None, None, ("clips", "tiles"), None),
            P(None, ("clips", "tiles")),
            P(None, ("clips", "tiles")),
            P(),
            P(),
        ),
        out_specs=(
            P(None, None, ("clips", "tiles"), None),
            P(None, None, ("clips", "tiles"), None),
        ),
        check_vma=False,
    )
```

```python
import functools

import jax
import jax.numpy as jnp
from jax import lax
from jax.experimental import pallas as pl
from jax.experimental.pallas import tpu as pltpu
from jax.sharding import PartitionSpec as P

BS = 8
REACH = 2
OFFSETS = tuple(o for o in range(-REACH, REACH + 1) if o != 0)


def leaky(value):
    return jnp.where(value >= 0, value, 0.1 * value)


def blockdiag(tile):
    blank = jnp.zeros(tile.shape, tile.dtype)
    return jnp.concatenate(
        [jnp.concatenate([tile, blank], axis=1), jnp.concatenate([blank, tile], axis=1)], axis=0
    )


def matmul_t(left, right):
    return lax.dot_general(
        left, right, (((1,), (1,)), ((), ())), preferred_element_type=jnp.float32
    )


def sweep_kernel(
    dims,
    x_ref,
    mf_ref,
    mb_ref,
    join_ref,
    conv_ref,
    ahead_ref,
    behind_ref,
    wj_ref,
    wc_ref,
    mine,
    theirs,
    table_v,
    table_s,
    cand,
    packed,
    landed,
    aligned,
    h_ref,
    z_ref,
    edge_out,
    edge_in,
    m_send,
    m_recv,
    f_send,
    f_recv,
    e_send,
    e_recv,
    t_sem,
):
    frame_count, rows, cols, channels, layers, devices = dims
    outs = (ahead_ref, behind_ref)
    lanes = 2 * channels
    width = cols // 2
    bc = cols // BS
    pairs = bc // 2
    cap = bc // (2 * REACH)
    sides = len(OFFSETS)
    kept = pairs + sides * cap // 2
    cell = BS * BS
    own = rows * width
    halo = layers * width
    me = lax.axis_index("tiles")

    def present(offset):
        return (me + offset >= 0) & (me + offset < devices)

    def remote(source, target, send, receive, offset):
        return pltpu.make_async_remote_copy(
            src_ref=source,
            dst_ref=target,
            send_sem=send,
            recv_sem=receive,
            device_id={"tiles": me + offset},
            device_id_type=pl.DeviceIdType.MESH,
        )

    def motion_copy(oi, slot):
        return remote(mine, theirs.at[slot], m_send.at[oi], m_recv.at[slot], OFFSETS[oi])

    def feature_copy(d, step, oi, slot):
        return remote(
            packed.at[d, step, oi], landed.at[d, step, slot],
            f_send.at[d, step, oi], f_recv.at[d, step, slot], OFFSETS[oi],
        )

    def edge_copy(d, step, side, slot):
        return remote(
            edge_out.at[d, step, side], edge_in.at[d, step, slot],
            e_send.at[d, step, side], e_recv.at[d, step, slot], 1 if side else -1,
        )

    barrier = pltpu.get_barrier_semaphore()
    for offset in OFFSETS:
        @pl.when(present(offset))
        def _():
            pl.semaphore_signal(
                barrier, inc=1, device_id={"tiles": me + offset},
                device_id_type=pl.DeviceIdType.MESH,
            )

    mine[...] = jnp.zeros(mine.shape, jnp.int32)
    for step in range(frame_count - 1):
        mine[step:step + 1, 0:bc] = mf_ref[step:step + 1, :]
        back = frame_count - 2 - step
        mine[frame_count - 1 + step:frame_count + step, 0:bc] = mb_ref[back:back + 1, :]

    for d in range(2):
        joined = join_ref[d]
        wj_ref[d, :, :lanes] = blockdiag(joined[:, :channels])
        wj_ref[d, :, lanes:] = blockdiag(joined[:, channels:])

        def build_layer(layer, carry):
            for tap in range(9):
                down, across = tap // 3, tap % 3
                wc_ref[
                    d, layer, across * lanes:(across + 1) * lanes, down * lanes:(down + 1) * lanes
                ] = blockdiag(conv_ref[d, layer, tap])
            return carry

        lax.fori_loop(0, layers, build_layer, 0)

    peers = jnp.minimum(me, REACH) + jnp.minimum(devices - 1 - me, REACH)
    pl.semaphore_wait(barrier, peers)

    for oi, offset in enumerate(OFFSETS):
        @pl.when(present(offset))
        def _():
            motion_copy(oi, sides - 1 - oi).start()

    lane = lax.broadcasted_iota(jnp.int32, mine.shape, 1)

    def prefix(flags):
        total = flags
        shift = 1
        while shift < bc:
            total = total + jnp.where(lane >= shift, pltpu.roll(total, shift, axis=1), 0)
            shift *= 2
        return total - flags

    def owned(motion, device):
        low = device * bc
        return (motion >= low) & (motion < low + bc) & (lane < bc)

    def own_code(local):
        return jnp.where(local < pairs, local, kept + local - pairs)

    def swapped(code):
        return jnp.where(code >= kept, code - kept, code + kept)

    def build_tables():
        motion = mine[...]
        picks = jnp.where(owned(motion, me), own_code(motion - me * bc), 0)
        for oi, offset in enumerate(OFFSETS):
            match = owned(motion, me + offset)
            rank = jnp.minimum(prefix(match.astype(jnp.int32)), cap - 1)
            base = pairs + oi * cap // 2
            code = jnp.where(rank < cap // 2, base + rank, kept + base + rank - cap // 2)
            picks = picks + jnp.where(match, code, 0)
        table_v[sides] = jnp.where(lane < pairs, picks, swapped(picks))
        for oi, offset in enumerate(OFFSETS):
            @pl.when(present(offset))
            def _():
                motion_copy(oi, oi).wait_send()
                motion_copy(oi, oi).wait_recv()
                wanted = theirs[oi]
                match = owned(wanted, me)
                rank = prefix(match.astype(jnp.int32))
                code = own_code(wanted - me * bc)
                gathered = jnp.zeros(mine.shape, jnp.int32)
                for slot in range(cap):
                    held = code if slot < cap // 2 else swapped(code)
                    value = jnp.where(match & (rank == slot), held, 0)
                    shift = 1
                    while shift < bc:
                        value = value + pltpu.roll(value, shift, axis=1)
                        shift *= 2
                    value = pltpu.roll(value, 1 + slot, axis=1)
                    gathered = jnp.where(lane == bc + slot, value, gathered)
                table_v[oi] = gathered

            @pl.when(jnp.logical_not(present(offset)))
            def _():
                table_v[oi] = jnp.zeros(mine.shape, jnp.int32)
        load = pltpu.make_async_copy(table_v, table_s, t_sem)
        load.start()
        load.wait()

    left_half = lax.broadcasted_iota(jnp.int32, (rows, BS, lanes), 2) < channels

    def keep(d, index, tile):
        cand[d, index] = tile
        cand[d, kept + index] = pltpu.roll(tile, channels, axis=2)

    def begin(d, t):
        @pl.when(t == 0)
        def _():
            aligned[d] = jnp.zeros(aligned.shape[1:], aligned.dtype)

        @pl.when(t > 0)
        def _():
            step = t - 1
            row = d * (frame_count - 1) + step
            for oi, offset in enumerate(OFFSETS):
                @pl.when(present(offset))
                def _():
                    feature_copy(d, step, oi, oi).wait_recv()
                    tiles = landed[d, step, oi].astype(jnp.float32)
                    tiles = tiles.reshape(cap // 2, BS, BS, lanes)
                    for pair in range(cap // 2):
                        keep(d, pairs + oi * cap // 2 + pair, tiles[pair])
            for j in range(pairs):
                low = table_s[sides, row, j]
                high = table_s[sides, row, pairs + j]
                aligned[d, :, j * BS:(j + 1) * BS, :] = jnp.where(
                    left_half, cand[d, low], cand[d, high]
                )

        now = t if d == 0 else frame_count - 1 - t
        both = jnp.concatenate(
            [aligned[d].reshape(own, lanes).astype(jnp.bfloat16), x_ref[now]], axis=1
        )
        first = matmul_t(both, wj_ref[d]).astype(jnp.bfloat16)
        edge_out[d, t, 0] = first[:halo]
        edge_out[d, t, 1] = first[own - halo:]
        for side in range(2):
            @pl.when(present(1 if side else -1))
            def _():
                edge_copy(d, t, side, 1 - side).start()
        h_ref[d, halo:halo + own, :] = first
        z_ref[d, 0, halo:halo + own, :] = leaky(first.astype(jnp.float32)).astype(jnp.bfloat16)

    def finish(d, t):
        for side in range(2):
            start = side * (halo + own)

            @pl.when(present(1 if side else -1))
            def _():
                edge_copy(d, t, side, side).wait_recv()
                edge = edge_in[d, t, side]
                h_ref[d, start:start + halo, :] = edge
                z_ref[d, 0, start:start + halo, :] = leaky(edge.astype(jnp.float32)).astype(
                    jnp.bfloat16
                )

            @pl.when(jnp.logical_not(present(1 if side else -1)))
            def _():
                h_ref[d, start:start + halo, :] = jnp.zeros((halo, lanes), jnp.bfloat16)
                z_ref[d, 0, start:start + halo, :] = jnp.zeros((halo, lanes), jnp.bfloat16)

        for layer in range(layers):
            out_rows = rows + 2 * (layers - 1 - layer)
            size = out_rows * width
            source = z_ref.at[d, layer % 2]
            target = z_ref.at[d, 1 - layer % 2]
            stack = jnp.concatenate(
                [source[(layer + k) * width:(layer + k) * width + size, :] for k in range(3)],
                axis=1,
            )
            summed = matmul_t(stack, wc_ref[d, layer])
            place = lax.broadcasted_iota(jnp.int32, (out_rows, BS, lanes), 1)
            lefts = lax.broadcasted_iota(jnp.int32, (out_rows, BS, lanes), 2) < channels
            before = pltpu.roll(summed[:, :lanes].reshape(out_rows, width, lanes), 1, axis=1)
            seam = before[:, :BS]
            crossed = jnp.where(lefts, 0.0, pltpu.roll(seam, channels, axis=2))
            before = jnp.concatenate(
                [jnp.where(place == 0, crossed, seam), before[:, BS:]], axis=1
            ).reshape(size, lanes)
            after = pltpu.roll(
                summed[:, 2 * lanes:].reshape(out_rows, width, lanes), width - 1, axis=1
            )
            seam = after[:, width - BS:]
            crossed = jnp.where(lefts, pltpu.roll(seam, channels, axis=2), 0.0)
            after = jnp.concatenate(
                [after[:, :width - BS], jnp.where(place == BS - 1, crossed, seam)], axis=1
            ).reshape(size, lanes)
            base = (layer + 1) * width
            total = h_ref[d, base:base + size, :].astype(jnp.float32) + summed[:, lanes:2 * lanes]
            rounded = (total + before + after).astype(jnp.bfloat16)
            if layer < layers - 1:
                h_ref[d, base:base + size, :] = rounded
                target[base:base + size, :] = leaky(rounded.astype(jnp.float32)).astype(jnp.bfloat16)
                outside = halo - base

                @pl.when(me == 0)
                def _():
                    target[base:halo, :] = jnp.zeros((outside, lanes), jnp.bfloat16)

                @pl.when(me == devices - 1)
                def _():
                    target[halo + own:halo + own + outside, :] = jnp.zeros(
                        (outside, lanes), jnp.bfloat16
                    )
            else:
                grid = rounded.astype(jnp.float32).reshape(rows, pairs, BS, lanes)
                for j in range(pairs):
                    keep(d, j, grid[:, j])
                now = t if d == 0 else frame_count - 1 - t
                outs[d][now] = rounded

        @pl.when(t < frame_count - 1)
        def _():
            row = d * (frame_count - 1) + t
            for oi, offset in enumerate(OFFSETS):
                @pl.when(present(offset))
                def _():
                    for pair in range(cap // 2):
                        low = table_s[oi, row, bc + pair]
                        high = table_s[oi, row, bc + cap // 2 + pair]
                        block = jnp.where(left_half, cand[d, low], cand[d, high])
                        packed[d, t, oi, pair * cell:(pair + 1) * cell, :] = block.reshape(
                            cell, lanes
                        ).astype(jnp.bfloat16)
                    feature_copy(d, t, oi, sides - 1 - oi).start()

    def frame_step(t, carry):
        begin(0, t)
        begin(1, t)

        @pl.when(t == 0)
        def _():
            build_tables()

        finish(0, t)
        finish(1, t)
        return carry

    lax.fori_loop(0, frame_count, frame_step, 0)

    for d in range(2):
        for step in range(frame_count):
            for side in range(2):
                @pl.when(present(1 if side else -1))
                def _():
                    edge_copy(d, step, side, side).wait_send()
            if step < frame_count - 1:
                for oi, offset in enumerate(OFFSETS):
                    @pl.when(present(offset))
                    def _():
                        feature_copy(d, step, oi, oi).wait_send()


def on_device(frames, motion_forward, motion_backward, join_weight, conv_weight):
    frame_count, channels, rows, cols = frames.shape
    layers = conv_weight.shape[1]
    devices = lax.axis_size("tiles")
    lanes = 2 * channels
    width = cols // 2
    own = rows * width
    halo = layers * width
    bc = rows // BS * (cols // BS)
    cap = bc // (2 * REACH)
    sides = len(OFFSETS)
    steps = frame_count - 1
    kept = bc // 2 + sides * cap // 2

    x = frames.reshape(frame_count, channels, rows, 2, width).transpose(0, 2, 4, 3, 1)
    x = x.reshape(frame_count, own, lanes)

    dims = (frame_count, rows, cols, channels, layers, devices)
    vmem = pl.BlockSpec(memory_space=pltpu.VMEM)
    result = jax.ShapeDtypeStruct((frame_count, own, lanes), jnp.bfloat16)
    outs = pl.pallas_call(
        functools.partial(sweep_kernel, dims),
        out_shape=(result, result),
        in_specs=[vmem] * 5,
        out_specs=(vmem, vmem),
        scratch_shapes=[
            pltpu.VMEM((2, lanes, 2 * lanes), jnp.bfloat16),
            pltpu.VMEM((2, layers, 3 * lanes, 3 * lanes), jnp.bfloat16),
            pltpu.VMEM((8, 128), jnp.int32),
            pltpu.VMEM((sides, 8, 128), jnp.int32),
            pltpu.VMEM((sides + 1, 8, 128), jnp.int32),
            pltpu.SMEM((sides + 1, 8, 128), jnp.int32),
            pltpu.VMEM((2, 2 * kept, BS, BS, lanes), jnp.float32),
            pltpu.VMEM((2, steps, sides, cap // 2 * BS * BS, lanes), jnp.bfloat16),
            pltpu.VMEM((2, steps, sides, cap // 2 * BS * BS, lanes), jnp.bfloat16),
            pltpu.VMEM((2, rows, width, lanes), jnp.float32),
            pltpu.VMEM((2, own + 2 * halo, lanes), jnp.bfloat16),
            pltpu.VMEM((2, 2, own + 2 * halo, lanes), jnp.bfloat16),
            pltpu.VMEM((2, frame_count, 2, halo, lanes), jnp.bfloat16),
            pltpu.VMEM((2, frame_count, 2, halo, lanes), jnp.bfloat16),
            pltpu.SemaphoreType.DMA((sides,)),
            pltpu.SemaphoreType.DMA((sides,)),
            pltpu.SemaphoreType.DMA((2, steps, sides)),
            pltpu.SemaphoreType.DMA((2, steps, sides)),
            pltpu.SemaphoreType.DMA((2, frame_count, 2)),
            pltpu.SemaphoreType.DMA((2, frame_count, 2)),
            pltpu.SemaphoreType.DMA,
        ],
        compiler_params=pltpu.CompilerParams(
            collective_id=0, has_side_effects=True, vmem_limit_bytes=56 * 1024 * 1024
        ),
    )(x, motion_forward, motion_backward, join_weight, conv_weight)

    def placed(out):
        out = out.reshape(frame_count, rows, width, 2, channels)
        return out.transpose(0, 4, 1, 3, 2).reshape(frame_count, channels, rows, cols)

    return placed(outs[0]), placed(outs[1])


def solution(mesh):
    return jax.shard_map(
        on_device,
        mesh=mesh,
        in_specs=(
            P(None, None, ("clips", "tiles"), None),
            P(None, ("clips", "tiles")),
            P(None, ("clips", "tiles")),
            P(),
            P(),
        ),
        out_specs=(
            P(None, None, ("clips", "tiles"), None),
            P(None, None, ("clips", "tiles"), None),
        ),
        check_vma=False,
    )
```

```python
import functools

import jax
import jax.numpy as jnp
from jax import lax
from jax.experimental import pallas as pl
from jax.experimental.pallas import tpu as pltpu
from jax.sharding import PartitionSpec as P

BS = 8
REACH = 2
OFFSETS = tuple(o for o in range(-REACH, REACH + 1) if o != 0)


def leaky(value):
    return jnp.where(value >= 0, value, 0.1 * value)


def blockdiag(tile):
    blank = jnp.zeros(tile.shape, tile.dtype)
    return jnp.concatenate(
        [jnp.concatenate([tile, blank], axis=1), jnp.concatenate([blank, tile], axis=1)], axis=0
    )


def matmul_t(left, right):
    return lax.dot_general(
        left, right, (((1,), (1,)), ((), ())), preferred_element_type=jnp.float32
    )


def sweep_kernel(
    dims,
    frames_ref,
    mf_ref,
    mb_ref,
    join_ref,
    conv_ref,
    ahead_ref,
    behind_ref,
    x_ref,
    flip,
    wj_ref,
    wc_ref,
    mine,
    theirs,
    table_v,
    table_s,
    cand,
    packed,
    landed,
    aligned,
    h_ref,
    z_ref,
    edge_out,
    edge_in,
    m_send,
    m_recv,
    f_send,
    f_recv,
    e_send,
    e_recv,
    t_sem,
):
    frame_count, rows, cols, channels, layers, devices = dims
    outs = (ahead_ref, behind_ref)
    lanes = 2 * channels
    width = cols // 2
    bc = cols // BS
    pairs = bc // 2
    cap = bc // (2 * REACH)
    sides = len(OFFSETS)
    kept = pairs + sides * cap // 2
    cell = BS * BS
    own = rows * width
    halo = layers * width
    me = lax.axis_index("tiles")

    def present(offset):
        return (me + offset >= 0) & (me + offset < devices)

    def remote(source, target, send, receive, offset):
        return pltpu.make_async_remote_copy(
            src_ref=source,
            dst_ref=target,
            send_sem=send,
            recv_sem=receive,
            device_id={"tiles": me + offset},
            device_id_type=pl.DeviceIdType.MESH,
        )

    def motion_copy(oi, slot):
        return remote(mine, theirs.at[slot], m_send.at[oi], m_recv.at[slot], OFFSETS[oi])

    def feature_copy(d, step, oi, slot):
        return remote(
            packed.at[d, step, oi], landed.at[d, step, slot],
            f_send.at[d, step, oi], f_recv.at[d, step, slot], OFFSETS[oi],
        )

    def edge_copy(d, step, side, slot):
        return remote(
            edge_out.at[d, step, side], edge_in.at[d, step, slot],
            e_send.at[d, step, side], e_recv.at[d, step, slot], 1 if side else -1,
        )

    barrier = pltpu.get_barrier_semaphore()
    for offset in OFFSETS:
        @pl.when(present(offset))
        def _():
            pl.semaphore_signal(
                barrier, inc=1, device_id={"tiles": me + offset},
                device_id_type=pl.DeviceIdType.MESH,
            )

    mine[...] = jnp.zeros(mine.shape, jnp.int32)
    for step in range(frame_count - 1):
        mine[step:step + 1, 0:bc] = mf_ref[step:step + 1, :]
        back = frame_count - 2 - step
        mine[frame_count - 1 + step:frame_count + step, 0:bc] = mb_ref[back:back + 1, :]

    for d in range(2):
        joined = join_ref[d]
        wj_ref[d, :, :lanes] = blockdiag(joined[:, :channels])
        wj_ref[d, :, lanes:] = blockdiag(joined[:, channels:])

        def build_layer(layer, carry):
            for tap in range(9):
                down, across = tap // 3, tap % 3
                wc_ref[
                    d, layer, across * lanes:(across + 1) * lanes, down * lanes:(down + 1) * lanes
                ] = blockdiag(conv_ref[d, layer, tap])
            return carry

        lax.fori_loop(0, layers, build_layer, 0)

    def picker(count):
        row = lax.broadcasted_iota(jnp.int32, (count, 2 * count), 0)
        column = lax.broadcasted_iota(jnp.int32, (count, 2 * count), 1)
        return ((column == row) | (column == row + count)).astype(jnp.bfloat16)

    def load_frame(f, carry):
        flip[0] = frames_ref[f].astype(jnp.float32).reshape(channels * rows, cols)
        first = lax.broadcasted_iota(jnp.int32, (channels, cols), 1) < width
        parts = []
        for r in range(rows):
            row = flip[0, pl.ds(r, channels, stride=rows), :]
            parts += [jnp.where(first, row, 0.0), jnp.where(first, 0.0, row)]
        moved = matmul_t(picker(width), jnp.concatenate(parts, axis=0).astype(jnp.bfloat16))
        for r in range(rows):
            x_ref[f, r * width:(r + 1) * width, :] = moved[:, r * lanes:(r + 1) * lanes].astype(
                jnp.bfloat16
            )
        return carry

    lax.fori_loop(0, frame_count, load_frame, 0)

    def emit(d, t):
        value = h_ref[d, halo:halo + own, :].astype(jnp.float32).reshape(rows, width, lanes)
        first = lax.broadcasted_iota(jnp.int32, value.shape, 2) < channels
        split = jnp.concatenate(
            [jnp.where(first, value, 0.0), jnp.where(first, 0.0, value)], axis=1
        ).reshape(rows * cols, lanes).astype(jnp.bfloat16)
        moved = matmul_t(picker(channels), split)
        for r in range(rows):
            flip[d, pl.ds(r, channels, stride=rows), :] = moved[:, r * cols:(r + 1) * cols]
        now = t if d == 0 else frame_count - 1 - t
        outs[d][now] = flip[d].reshape(channels, rows, cols).astype(jnp.bfloat16)

    peers = jnp.minimum(me, REACH) + jnp.minimum(devices - 1 - me, REACH)
    pl.semaphore_wait(barrier, peers)

    for oi, offset in enumerate(OFFSETS):
        @pl.when(present(offset))
        def _():
            motion_copy(oi, sides - 1 - oi).start()

    lane = lax.broadcasted_iota(jnp.int32, mine.shape, 1)

    def prefix(flags):
        total = flags
        shift = 1
        while shift < bc:
            total = total + jnp.where(lane >= shift, pltpu.roll(total, shift, axis=1), 0)
            shift *= 2
        return total - flags

    def owned(motion, device):
        low = device * bc
        return (motion >= low) & (motion < low + bc) & (lane < bc)

    def own_code(local):
        return jnp.where(local < pairs, local, kept + local - pairs)

    def swapped(code):
        return jnp.where(code >= kept, code - kept, code + kept)

    def build_tables():
        motion = mine[...]
        picks = jnp.where(owned(motion, me), own_code(motion - me * bc), 0)
        for oi, offset in enumerate(OFFSETS):
            match = owned(motion, me + offset)
            rank = jnp.minimum(prefix(match.astype(jnp.int32)), cap - 1)
            base = pairs + oi * cap // 2
            code = jnp.where(rank < cap // 2, base + rank, kept + base + rank - cap // 2)
            picks = picks + jnp.where(match, code, 0)
        table_v[sides] = jnp.where(lane < pairs, picks, swapped(picks))
        for oi, offset in enumerate(OFFSETS):
            @pl.when(present(offset))
            def _():
                motion_copy(oi, oi).wait_send()
                motion_copy(oi, oi).wait_recv()
                wanted = theirs[oi]
                match = owned(wanted, me)
                rank = prefix(match.astype(jnp.int32))
                code = own_code(wanted - me * bc)
                gathered = jnp.zeros(mine.shape, jnp.int32)
                for slot in range(cap):
                    held = code if slot < cap // 2 else swapped(code)
                    value = jnp.where(match & (rank == slot), held, 0)
                    shift = 1
                    while shift < bc:
                        value = value + pltpu.roll(value, shift, axis=1)
                        shift *= 2
                    value = pltpu.roll(value, 1 + slot, axis=1)
                    gathered = jnp.where(lane == bc + slot, value, gathered)
                table_v[oi] = gathered

            @pl.when(jnp.logical_not(present(offset)))
            def _():
                table_v[oi] = jnp.zeros(mine.shape, jnp.int32)
        load = pltpu.make_async_copy(table_v, table_s, t_sem)
        load.start()
        load.wait()

    left_half = lax.broadcasted_iota(jnp.int32, (rows, BS, lanes), 2) < channels

    def keep(d, index, tile):
        cand[d, index] = tile
        cand[d, kept + index] = pltpu.roll(tile, channels, axis=2)

    def begin(d, t):
        @pl.when(t == 0)
        def _():
            aligned[d] = jnp.zeros(aligned.shape[1:], aligned.dtype)

        @pl.when(t > 0)
        def _():
            step = t - 1
            row = d * (frame_count - 1) + step
            for oi, offset in enumerate(OFFSETS):
                @pl.when(present(offset))
                def _():
                    feature_copy(d, step, oi, oi).wait_recv()
                    tiles = landed[d, step, oi].astype(jnp.float32)
                    tiles = tiles.reshape(cap // 2, BS, BS, lanes)
                    for pair in range(cap // 2):
                        keep(d, pairs + oi * cap // 2 + pair, tiles[pair])
            for j in range(pairs):
                low = table_s[sides, row, j]
                high = table_s[sides, row, pairs + j]
                aligned[d, :, j * BS:(j + 1) * BS, :] = jnp.where(
                    left_half, cand[d, low], cand[d, high]
                )

        now = t if d == 0 else frame_count - 1 - t
        both = jnp.concatenate(
            [aligned[d].reshape(own, lanes).astype(jnp.bfloat16), x_ref[now]], axis=1
        )
        first = matmul_t(both, wj_ref[d]).astype(jnp.bfloat16)
        edge_out[d, t, 0] = first[:halo]
        edge_out[d, t, 1] = first[own - halo:]
        for side in range(2):
            @pl.when(present(1 if side else -1))
            def _():
                edge_copy(d, t, side, 1 - side).start()
        h_ref[d, halo:halo + own, :] = first
        z_ref[d, 0, halo:halo + own, :] = leaky(first.astype(jnp.float32)).astype(jnp.bfloat16)

    def finish(d, t):
        for side in range(2):
            start = side * (halo + own)

            @pl.when(present(1 if side else -1))
            def _():
                edge_copy(d, t, side, side).wait_recv()
                edge = edge_in[d, t, side]
                h_ref[d, start:start + halo, :] = edge
                z_ref[d, 0, start:start + halo, :] = leaky(edge.astype(jnp.float32)).astype(
                    jnp.bfloat16
                )

            @pl.when(jnp.logical_not(present(1 if side else -1)))
            def _():
                h_ref[d, start:start + halo, :] = jnp.zeros((halo, lanes), jnp.bfloat16)
                z_ref[d, 0, start:start + halo, :] = jnp.zeros((halo, lanes), jnp.bfloat16)

        for layer in range(layers):
            out_rows = rows + 2 * (layers - 1 - layer)
            size = out_rows * width
            source = z_ref.at[d, layer % 2]
            target = z_ref.at[d, 1 - layer % 2]
            stack = jnp.concatenate(
                [source[(layer + k) * width:(layer + k) * width + size, :] for k in range(3)],
                axis=1,
            )
            summed = matmul_t(stack, wc_ref[d, layer])
            place = lax.broadcasted_iota(jnp.int32, (out_rows, BS, lanes), 1)
            lefts = lax.broadcasted_iota(jnp.int32, (out_rows, BS, lanes), 2) < channels
            before = pltpu.roll(summed[:, :lanes].reshape(out_rows, width, lanes), 1, axis=1)
            seam = before[:, :BS]
            crossed = jnp.where(lefts, 0.0, pltpu.roll(seam, channels, axis=2))
            before = jnp.concatenate(
                [jnp.where(place == 0, crossed, seam), before[:, BS:]], axis=1
            ).reshape(size, lanes)
            after = pltpu.roll(
                summed[:, 2 * lanes:].reshape(out_rows, width, lanes), width - 1, axis=1
            )
            seam = after[:, width - BS:]
            crossed = jnp.where(lefts, pltpu.roll(seam, channels, axis=2), 0.0)
            after = jnp.concatenate(
                [after[:, :width - BS], jnp.where(place == BS - 1, crossed, seam)], axis=1
            ).reshape(size, lanes)
            base = (layer + 1) * width
            total = h_ref[d, base:base + size, :].astype(jnp.float32) + summed[:, lanes:2 * lanes]
            rounded = (total + before + after).astype(jnp.bfloat16)
            if layer < layers - 1:
                h_ref[d, base:base + size, :] = rounded
                target[base:base + size, :] = leaky(rounded.astype(jnp.float32)).astype(jnp.bfloat16)
                outside = halo - base

                @pl.when(me == 0)
                def _():
                    target[base:halo, :] = jnp.zeros((outside, lanes), jnp.bfloat16)

                @pl.when(me == devices - 1)
                def _():
                    target[halo + own:halo + own + outside, :] = jnp.zeros(
                        (outside, lanes), jnp.bfloat16
                    )
            else:
                grid = rounded.astype(jnp.float32).reshape(rows, pairs, BS, lanes)
                for j in range(pairs):
                    keep(d, j, grid[:, j])
                h_ref[d, base:base + size, :] = rounded

        @pl.when(t < frame_count - 1)
        def _():
            row = d * (frame_count - 1) + t
            for oi, offset in enumerate(OFFSETS):
                @pl.when(present(offset))
                def _():
                    for pair in range(cap // 2):
                        low = table_s[oi, row, bc + pair]
                        high = table_s[oi, row, bc + cap // 2 + pair]
                        block = jnp.where(left_half, cand[d, low], cand[d, high])
                        packed[d, t, oi, pair * cell:(pair + 1) * cell, :] = block.reshape(
                            cell, lanes
                        ).astype(jnp.bfloat16)
                    feature_copy(d, t, oi, sides - 1 - oi).start()

    def frame_step(t, carry):
        begin(0, t)
        begin(1, t)

        @pl.when(t == 0)
        def _():
            build_tables()

        finish(0, t)
        finish(1, t)
        emit(0, t)
        emit(1, t)
        return carry

    lax.fori_loop(0, frame_count, frame_step, 0)

    for d in range(2):
        for step in range(frame_count):
            for side in range(2):
                @pl.when(present(1 if side else -1))
                def _():
                    edge_copy(d, step, side, side).wait_send()
            if step < frame_count - 1:
                for oi, offset in enumerate(OFFSETS):
                    @pl.when(present(offset))
                    def _():
                        feature_copy(d, step, oi, oi).wait_send()


def on_device(frames, motion_forward, motion_backward, join_weight, conv_weight):
    frame_count, channels, rows, cols = frames.shape
    layers = conv_weight.shape[1]
    devices = lax.axis_size("tiles")
    lanes = 2 * channels
    width = cols // 2
    own = rows * width
    halo = layers * width
    bc = rows // BS * (cols // BS)
    cap = bc // (2 * REACH)
    sides = len(OFFSETS)
    steps = frame_count - 1
    kept = bc // 2 + sides * cap // 2

    dims = (frame_count, rows, cols, channels, layers, devices)
    vmem = pl.BlockSpec(memory_space=pltpu.VMEM)
    result = jax.ShapeDtypeStruct(frames.shape, jnp.bfloat16)
    return pl.pallas_call(
        functools.partial(sweep_kernel, dims),
        out_shape=(result, result),
        in_specs=[vmem] * 5,
        out_specs=(vmem, vmem),
        scratch_shapes=[
            pltpu.VMEM((frame_count, own, lanes), jnp.bfloat16),
            pltpu.VMEM((2, channels * rows, cols), jnp.float32),
            pltpu.VMEM((2, lanes, 2 * lanes), jnp.bfloat16),
            pltpu.VMEM((2, layers, 3 * lanes, 3 * lanes), jnp.bfloat16),
            pltpu.VMEM((8, 128), jnp.int32),
            pltpu.VMEM((sides, 8, 128), jnp.int32),
            pltpu.VMEM((sides + 1, 8, 128), jnp.int32),
            pltpu.SMEM((sides + 1, 8, 128), jnp.int32),
            pltpu.VMEM((2, 2 * kept, BS, BS, lanes), jnp.float32),
            pltpu.VMEM((2, steps, sides, cap // 2 * BS * BS, lanes), jnp.bfloat16),
            pltpu.VMEM((2, steps, sides, cap // 2 * BS * BS, lanes), jnp.bfloat16),
            pltpu.VMEM((2, rows, width, lanes), jnp.float32),
            pltpu.VMEM((2, own + 2 * halo, lanes), jnp.bfloat16),
            pltpu.VMEM((2, 2, own + 2 * halo, lanes), jnp.bfloat16),
            pltpu.VMEM((2, frame_count, 2, halo, lanes), jnp.bfloat16),
            pltpu.VMEM((2, frame_count, 2, halo, lanes), jnp.bfloat16),
            pltpu.SemaphoreType.DMA((sides,)),
            pltpu.SemaphoreType.DMA((sides,)),
            pltpu.SemaphoreType.DMA((2, steps, sides)),
            pltpu.SemaphoreType.DMA((2, steps, sides)),
            pltpu.SemaphoreType.DMA((2, frame_count, 2)),
            pltpu.SemaphoreType.DMA((2, frame_count, 2)),
            pltpu.SemaphoreType.DMA,
        ],
        compiler_params=pltpu.CompilerParams(
            collective_id=0, has_side_effects=True, vmem_limit_bytes=56 * 1024 * 1024
        ),
    )(frames, motion_forward, motion_backward, join_weight, conv_weight)


def solution(mesh):
    return jax.shard_map(
        on_device,
        mesh=mesh,
        in_specs=(
            P(None, None, ("clips", "tiles"), None),
            P(None, ("clips", "tiles")),
            P(None, ("clips", "tiles")),
            P(),
            P(),
        ),
        out_specs=(
            P(None, None, ("clips", "tiles"), None),
            P(None, None, ("clips", "tiles"), None),
        ),
        check_vma=False,
    )
```

```python
import functools

import jax
import jax.numpy as jnp
from jax import lax
from jax.experimental import pallas as pl
from jax.experimental.pallas import tpu as pltpu
from jax.sharding import PartitionSpec as P

BS = 8
REACH = 2
OFFSETS = tuple(o for o in range(-REACH, REACH + 1) if o != 0)


def leaky(value):
    return jnp.where(value >= 0, value, 0.1 * value)


def blockdiag(tile):
    blank = jnp.zeros(tile.shape, tile.dtype)
    return jnp.concatenate(
        [jnp.concatenate([tile, blank], axis=1), jnp.concatenate([blank, tile], axis=1)], axis=0
    )


def matmul_t(left, right):
    return lax.dot_general(
        left, right, (((1,), (1,)), ((), ())), preferred_element_type=jnp.float32
    )


def sweep_kernel(
    dims,
    frames_ref,
    mf_ref,
    mb_ref,
    join_ref,
    conv_ref,
    ahead_ref,
    behind_ref,
    x_ref,
    flip,
    wj_ref,
    wc_ref,
    mine,
    theirs,
    table_v,
    table_s,
    cand,
    packed,
    landed,
    aligned,
    h_ref,
    z_ref,
    edge_out,
    edge_in,
    m_send,
    m_recv,
    f_send,
    f_recv,
    e_send,
    e_recv,
    t_sem,
):
    frame_count, rows, cols, channels, layers, devices = dims
    outs = (ahead_ref, behind_ref)
    lanes = 2 * channels
    width = cols // 2
    bc = cols // BS
    pairs = bc // 2
    cap = bc // (2 * REACH)
    sides = len(OFFSETS)
    kept = pairs + sides * cap // 2
    cell = BS * BS
    own = rows * width
    halo = layers * width
    me = lax.axis_index("tiles")

    def present(offset):
        return (me + offset >= 0) & (me + offset < devices)

    def remote(source, target, send, receive, offset):
        return pltpu.make_async_remote_copy(
            src_ref=source,
            dst_ref=target,
            send_sem=send,
            recv_sem=receive,
            device_id={"tiles": me + offset},
            device_id_type=pl.DeviceIdType.MESH,
        )

    def motion_copy(oi, slot):
        return remote(mine, theirs.at[slot], m_send.at[oi], m_recv.at[slot], OFFSETS[oi])

    def feature_copy(d, step, oi, slot):
        return remote(
            packed.at[d, step, oi], landed.at[d, step, slot],
            f_send.at[d, step, oi], f_recv.at[d, step, slot], OFFSETS[oi],
        )

    def edge_copy(d, step, side, slot):
        return remote(
            edge_out.at[d, step, side], edge_in.at[d, step, slot],
            e_send.at[d, step, side], e_recv.at[d, step, slot], 1 if side else -1,
        )

    barrier = pltpu.get_barrier_semaphore()
    for offset in OFFSETS:
        @pl.when(present(offset))
        def _():
            pl.semaphore_signal(
                barrier, inc=1, device_id={"tiles": me + offset},
                device_id_type=pl.DeviceIdType.MESH,
            )

    mine[...] = jnp.zeros(mine.shape, jnp.int32)
    for step in range(frame_count - 1):
        mine[step:step + 1, 0:bc] = mf_ref[step:step + 1, :]
        back = frame_count - 2 - step
        mine[frame_count - 1 + step:frame_count + step, 0:bc] = mb_ref[back:back + 1, :]

    identity = (
        lax.broadcasted_iota(jnp.int32, (channels, channels), 0)
        == lax.broadcasted_iota(jnp.int32, (channels, channels), 1)
    ).astype(jnp.bfloat16)
    for d in range(2):
        joined = join_ref[d]
        wj_ref[d, :, :lanes] = blockdiag(joined[:, :channels])
        wj_ref[d, :, lanes:] = blockdiag(joined[:, channels:])

        def build_layer(layer, carry):
            stacked = conv_ref[d, layer].reshape(9 * channels, channels)
            turned = matmul_t(identity, stacked).astype(jnp.bfloat16)
            blank = jnp.zeros((channels, channels), jnp.bfloat16)

            def tap(down, across):
                start = (3 * down + across) * channels
                return turned[:, start:start + channels]

            for side in range(2):
                order = (0, 1, 2, None) if side == 0 else (1, 0, None, 2)
                depth = (0, 1, 2, None) if side == 0 else (0, 1, None, 2)
                for k, down in enumerate(depth):
                    wc_ref[d, layer, side, k * channels:(k + 1) * channels, :] = jnp.concatenate(
                        [
                            blank if down is None or across is None else tap(down, across)
                            for across in order
                        ],
                        axis=1,
                    )
            return carry

        lax.fori_loop(0, layers, build_layer, 0)

    def picker(count):
        row = lax.broadcasted_iota(jnp.int32, (count, 2 * count), 0)
        column = lax.broadcasted_iota(jnp.int32, (count, 2 * count), 1)
        return ((column == row) | (column == row + count)).astype(jnp.bfloat16)

    def load_frame(f, carry):
        flip[0] = frames_ref[f].astype(jnp.float32).reshape(channels * rows, cols)
        first = lax.broadcasted_iota(jnp.int32, (channels, cols), 1) < width
        parts = []
        for r in range(rows):
            row = flip[0, pl.ds(r, channels, stride=rows), :]
            parts += [jnp.where(first, row, 0.0), jnp.where(first, 0.0, row)]
        moved = matmul_t(picker(width), jnp.concatenate(parts, axis=0).astype(jnp.bfloat16))
        for r in range(rows):
            x_ref[f, r * width:(r + 1) * width, :] = moved[:, r * lanes:(r + 1) * lanes].astype(
                jnp.bfloat16
            )
        return carry

    lax.fori_loop(0, frame_count, load_frame, 0)

    def emit(d, t):
        value = h_ref[d, halo:halo + own, :].astype(jnp.float32).reshape(rows, width, lanes)
        first = lax.broadcasted_iota(jnp.int32, value.shape, 2) < channels
        split = jnp.concatenate(
            [jnp.where(first, value, 0.0), jnp.where(first, 0.0, value)], axis=1
        ).reshape(rows * cols, lanes).astype(jnp.bfloat16)
        moved = matmul_t(picker(channels), split)
        for r in range(rows):
            flip[d, pl.ds(r, channels, stride=rows), :] = moved[:, r * cols:(r + 1) * cols]
        now = t if d == 0 else frame_count - 1 - t
        outs[d][now] = flip[d].reshape(channels, rows, cols).astype(jnp.bfloat16)

    peers = jnp.minimum(me, REACH) + jnp.minimum(devices - 1 - me, REACH)
    pl.semaphore_wait(barrier, peers)

    for oi, offset in enumerate(OFFSETS):
        @pl.when(present(offset))
        def _():
            motion_copy(oi, sides - 1 - oi).start()

    lane = lax.broadcasted_iota(jnp.int32, mine.shape, 1)

    def prefix(flags):
        total = flags
        shift = 1
        while shift < bc:
            total = total + jnp.where(lane >= shift, pltpu.roll(total, shift, axis=1), 0)
            shift *= 2
        return total - flags

    def owned(motion, device):
        low = device * bc
        return (motion >= low) & (motion < low + bc) & (lane < bc)

    def own_code(local):
        return jnp.where(local < pairs, local, kept + local - pairs)

    def swapped(code):
        return jnp.where(code >= kept, code - kept, code + kept)

    def build_tables():
        motion = mine[...]
        picks = jnp.where(owned(motion, me), own_code(motion - me * bc), 0)
        for oi, offset in enumerate(OFFSETS):
            match = owned(motion, me + offset)
            rank = jnp.minimum(prefix(match.astype(jnp.int32)), cap - 1)
            base = pairs + oi * cap // 2
            code = jnp.where(rank < cap // 2, base + rank, kept + base + rank - cap // 2)
            picks = picks + jnp.where(match, code, 0)
        table_v[sides] = jnp.where(lane < pairs, picks, swapped(picks))
        for oi, offset in enumerate(OFFSETS):
            @pl.when(present(offset))
            def _():
                motion_copy(oi, oi).wait_send()
                motion_copy(oi, oi).wait_recv()
                wanted = theirs[oi]
                match = owned(wanted, me)
                rank = prefix(match.astype(jnp.int32))
                code = own_code(wanted - me * bc)
                gathered = jnp.zeros(mine.shape, jnp.int32)
                for slot in range(cap):
                    held = code if slot < cap // 2 else swapped(code)
                    value = jnp.where(match & (rank == slot), held, 0)
                    shift = 1
                    while shift < bc:
                        value = value + pltpu.roll(value, shift, axis=1)
                        shift *= 2
                    value = pltpu.roll(value, 1 + slot, axis=1)
                    gathered = jnp.where(lane == bc + slot, value, gathered)
                table_v[oi] = gathered

            @pl.when(jnp.logical_not(present(offset)))
            def _():
                table_v[oi] = jnp.zeros(mine.shape, jnp.int32)
        load = pltpu.make_async_copy(table_v, table_s, t_sem)
        load.start()
        load.wait()

    left_half = lax.broadcasted_iota(jnp.int32, (rows, BS, lanes), 2) < channels

    def keep(d, index, tile):
        cand[d, index] = tile
        cand[d, kept + index] = pltpu.roll(tile, channels, axis=2)

    def activate(d, slot, start, value):
        size = value.shape[0]
        z_ref[d, slot, 0, start:start + size, :] = value.astype(jnp.bfloat16)
        z_ref[d, slot, 1, start:start + size, :] = pltpu.roll(value, channels, axis=1).astype(
            jnp.bfloat16
        )

    def begin(d, t):
        @pl.when(t == 0)
        def _():
            aligned[d] = jnp.zeros(aligned.shape[1:], aligned.dtype)

        @pl.when(t > 0)
        def _():
            step = t - 1
            row = d * (frame_count - 1) + step
            for oi, offset in enumerate(OFFSETS):
                @pl.when(present(offset))
                def _():
                    feature_copy(d, step, oi, oi).wait_recv()
                    tiles = landed[d, step, oi].astype(jnp.float32)
                    tiles = tiles.reshape(cap // 2, BS, BS, lanes)
                    for pair in range(cap // 2):
                        keep(d, pairs + oi * cap // 2 + pair, tiles[pair])
            for j in range(pairs):
                low = table_s[sides, row, j]
                high = table_s[sides, row, pairs + j]
                aligned[d, :, j * BS:(j + 1) * BS, :] = jnp.where(
                    left_half, cand[d, low], cand[d, high]
                )

        now = t if d == 0 else frame_count - 1 - t
        both = jnp.concatenate(
            [aligned[d].reshape(own, lanes).astype(jnp.bfloat16), x_ref[now]], axis=1
        )
        first = matmul_t(both, wj_ref[d]).astype(jnp.bfloat16)
        edge_out[d, t, 0] = first[:halo]
        edge_out[d, t, 1] = first[own - halo:]
        for side in range(2):
            @pl.when(present(1 if side else -1))
            def _():
                edge_copy(d, t, side, 1 - side).start()
        h_ref[d, halo:halo + own, :] = first
        activate(d, 0, halo, leaky(first.astype(jnp.float32)))

    top_inside = (me > 0).astype(jnp.float32)
    bottom_inside = (me < devices - 1).astype(jnp.float32)

    def finish(d, t):
        for side in range(2):
            start = side * (halo + own)

            @pl.when(present(1 if side else -1))
            def _():
                edge_copy(d, t, side, side).wait_recv()
                edge = edge_in[d, t, side]
                h_ref[d, start:start + halo, :] = edge
                activate(d, 0, start, leaky(edge.astype(jnp.float32)))

            @pl.when(jnp.logical_not(present(1 if side else -1)))
            def _():
                h_ref[d, start:start + halo, :] = jnp.zeros((halo, lanes), jnp.bfloat16)
                for swap in range(2):
                    z_ref[d, 0, swap, start:start + halo, :] = jnp.zeros(
                        (halo, lanes), jnp.bfloat16
                    )

        for layer in range(layers):
            out_rows = rows + 2 * (layers - 1 - layer)
            size = out_rows * width
            plain = z_ref.at[d, layer % 2, 0]
            turned = z_ref.at[d, layer % 2, 1]
            rows0 = pl.ds(layer * width, size)
            rows1 = pl.ds((layer + 1) * width, size)
            below = plain[(layer + 2) * width:(layer + 2) * width + size, :]
            low = lax.broadcasted_iota(jnp.int32, (size, lanes), 1) < channels
            upper = jnp.where(low, plain[rows0, :], turned[rows1, :])
            lower = jnp.where(low, turned[rows0, :], plain[rows1, :])
            one = jnp.dot(
                jnp.concatenate([upper, below], axis=1), wc_ref[d, layer, 0],
                preferred_element_type=jnp.float32,
            )
            two = jnp.dot(
                jnp.concatenate([lower, below], axis=1), wc_ref[d, layer, 1],
                preferred_element_type=jnp.float32,
            )
            tap0 = jnp.where(low, one[:, :lanes], two[:, :lanes])
            tap1 = pltpu.roll(jnp.where(low, two[:, :lanes], one[:, :lanes]), channels, axis=1)
            tap2 = jnp.where(low, one[:, lanes:], two[:, lanes:])
            place = lax.broadcasted_iota(jnp.int32, (out_rows, BS, lanes), 1)
            lefts = lax.broadcasted_iota(jnp.int32, (out_rows, BS, lanes), 2) < channels
            before = pltpu.roll(tap0.reshape(out_rows, width, lanes), 1, axis=1)
            seam = before[:, :BS]
            crossed = jnp.where(lefts, 0.0, pltpu.roll(seam, channels, axis=2))
            before = jnp.concatenate(
                [jnp.where(place == 0, crossed, seam), before[:, BS:]], axis=1
            ).reshape(size, lanes)
            after = pltpu.roll(tap2.reshape(out_rows, width, lanes), width - 1, axis=1)
            seam = after[:, width - BS:]
            crossed = jnp.where(lefts, pltpu.roll(seam, channels, axis=2), 0.0)
            after = jnp.concatenate(
                [after[:, :width - BS], jnp.where(place == BS - 1, crossed, seam)], axis=1
            ).reshape(size, lanes)
            base = (layer + 1) * width
            total = h_ref[d, base:base + size, :].astype(jnp.float32) + tap1
            rounded = (total + before + after).astype(jnp.bfloat16)
            if layer < layers - 1:
                h_ref[d, base:base + size, :] = rounded
                active = leaky(rounded.astype(jnp.float32))
                outside = halo - base
                active = jnp.concatenate(
                    [
                        active[:outside] * top_inside,
                        active[outside:size - outside],
                        active[size - outside:] * bottom_inside,
                    ],
                    axis=0,
                )
                activate(d, 1 - layer % 2, base, active)
            else:
                grid = rounded.astype(jnp.float32).reshape(rows, pairs, BS, lanes)
                for j in range(pairs):
                    keep(d, j, grid[:, j])
                h_ref[d, base:base + size, :] = rounded

        @pl.when(t < frame_count - 1)
        def _():
            row = d * (frame_count - 1) + t
            for oi, offset in enumerate(OFFSETS):
                @pl.when(present(offset))
                def _():
                    for pair in range(cap // 2):
                        low = table_s[oi, row, bc + pair]
                        high = table_s[oi, row, bc + cap // 2 + pair]
                        block = jnp.where(left_half, cand[d, low], cand[d, high])
                        packed[d, t, oi, pair * cell:(pair + 1) * cell, :] = block.reshape(
                            cell, lanes
                        ).astype(jnp.bfloat16)
                    feature_copy(d, t, oi, sides - 1 - oi).start()

    def frame_step(t, carry):
        begin(0, t)
        begin(1, t)

        @pl.when(t == 0)
        def _():
            build_tables()

        finish(0, t)
        finish(1, t)
        emit(0, t)
        emit(1, t)
        return carry

    lax.fori_loop(0, frame_count, frame_step, 0)

    for d in range(2):
        for step in range(frame_count):
            for side in range(2):
                @pl.when(present(1 if side else -1))
                def _():
                    edge_copy(d, step, side, side).wait_send()
            if step < frame_count - 1:
                for oi, offset in enumerate(OFFSETS):
                    @pl.when(present(offset))
                    def _():
                        feature_copy(d, step, oi, oi).wait_send()


def on_device(frames, motion_forward, motion_backward, join_weight, conv_weight):
    frame_count, channels, rows, cols = frames.shape
    layers = conv_weight.shape[1]
    devices = lax.axis_size("tiles")
    lanes = 2 * channels
    width = cols // 2
    own = rows * width
    halo = layers * width
    bc = rows // BS * (cols // BS)
    cap = bc // (2 * REACH)
    sides = len(OFFSETS)
    steps = frame_count - 1
    kept = bc // 2 + sides * cap // 2

    dims = (frame_count, rows, cols, channels, layers, devices)
    vmem = pl.BlockSpec(memory_space=pltpu.VMEM)
    result = jax.ShapeDtypeStruct(frames.shape, jnp.bfloat16)
    return pl.pallas_call(
        functools.partial(sweep_kernel, dims),
        out_shape=(result, result),
        in_specs=[vmem] * 5,
        out_specs=(vmem, vmem),
        scratch_shapes=[
            pltpu.VMEM((frame_count, own, lanes), jnp.bfloat16),
            pltpu.VMEM((2, channels * rows, cols), jnp.float32),
            pltpu.VMEM((2, lanes, 2 * lanes), jnp.bfloat16),
            pltpu.VMEM((2, layers, 2, 2 * lanes, 2 * lanes), jnp.bfloat16),
            pltpu.VMEM((8, 128), jnp.int32),
            pltpu.VMEM((sides, 8, 128), jnp.int32),
            pltpu.VMEM((sides + 1, 8, 128), jnp.int32),
            pltpu.SMEM((sides + 1, 8, 128), jnp.int32),
            pltpu.VMEM((2, 2 * kept, BS, BS, lanes), jnp.float32),
            pltpu.VMEM((2, steps, sides, cap // 2 * BS * BS, lanes), jnp.bfloat16),
            pltpu.VMEM((2, steps, sides, cap // 2 * BS * BS, lanes), jnp.bfloat16),
            pltpu.VMEM((2, rows, width, lanes), jnp.float32),
            pltpu.VMEM((2, own + 2 * halo, lanes), jnp.bfloat16),
            pltpu.VMEM((2, 2, 2, own + 2 * halo, lanes), jnp.bfloat16),
            pltpu.VMEM((2, frame_count, 2, halo, lanes), jnp.bfloat16),
            pltpu.VMEM((2, frame_count, 2, halo, lanes), jnp.bfloat16),
            pltpu.SemaphoreType.DMA((sides,)),
            pltpu.SemaphoreType.DMA((sides,)),
            pltpu.SemaphoreType.DMA((2, steps, sides)),
            pltpu.SemaphoreType.DMA((2, steps, sides)),
            pltpu.SemaphoreType.DMA((2, frame_count, 2)),
            pltpu.SemaphoreType.DMA((2, frame_count, 2)),
            pltpu.SemaphoreType.DMA,
        ],
        compiler_params=pltpu.CompilerParams(
            collective_id=0, has_side_effects=True, vmem_limit_bytes=56 * 1024 * 1024
        ),
    )(frames, motion_forward, motion_backward, join_weight, conv_weight)


def solution(mesh):
    return jax.shard_map(
        on_device,
        mesh=mesh,
        in_specs=(
            P(None, None, ("clips", "tiles"), None),
            P(None, ("clips", "tiles")),
            P(None, ("clips", "tiles")),
            P(),
            P(),
        ),
        out_specs=(
            P(None, None, ("clips", "tiles"), None),
            P(None, None, ("clips", "tiles"), None),
        ),
        check_vma=False,
    )
```

```python
import functools

import jax
import jax.numpy as jnp
from jax import lax
from jax.experimental import pallas as pl
from jax.experimental.pallas import tpu as pltpu
from jax.sharding import PartitionSpec as P

BS = 8
REACH = 2
OFFSETS = tuple(o for o in range(-REACH, REACH + 1) if o != 0)


def leaky(value):
    return jnp.where(value >= 0, value, 0.1 * value)


def blockdiag(tile):
    blank = jnp.zeros(tile.shape, tile.dtype)
    return jnp.concatenate(
        [jnp.concatenate([tile, blank], axis=1), jnp.concatenate([blank, tile], axis=1)], axis=0
    )


def matmul_t(left, right):
    return lax.dot_general(
        left, right, (((1,), (1,)), ((), ())), preferred_element_type=jnp.float32
    )


def sweep_kernel(
    dims,
    frames_ref,
    mf_ref,
    mb_ref,
    join_ref,
    conv_ref,
    ahead_ref,
    behind_ref,
    x_ref,
    flip,
    wj_ref,
    wc_ref,
    mine,
    theirs,
    table_v,
    table_s,
    cand,
    packed,
    landed,
    aligned,
    h_ref,
    z_ref,
    edge_out,
    edge_in,
    m_send,
    m_recv,
    f_send,
    f_recv,
    e_send,
    e_recv,
    t_sem,
):
    frame_count, rows, cols, channels, layers, devices = dims
    outs = (ahead_ref, behind_ref)
    lanes = 2 * channels
    width = cols // 2
    bc = cols // BS
    pairs = bc // 2
    cap = bc // (2 * REACH)
    sides = len(OFFSETS)
    kept = pairs + sides * cap // 2
    cell = BS * BS
    own = rows * width
    halo = layers * width
    me = lax.axis_index("tiles")

    def present(offset):
        return (me + offset >= 0) & (me + offset < devices)

    def remote(source, target, send, receive, offset):
        return pltpu.make_async_remote_copy(
            src_ref=source,
            dst_ref=target,
            send_sem=send,
            recv_sem=receive,
            device_id={"tiles": me + offset},
            device_id_type=pl.DeviceIdType.MESH,
        )

    def motion_copy(oi, slot):
        return remote(mine, theirs.at[slot], m_send.at[oi], m_recv.at[slot], OFFSETS[oi])

    def feature_copy(d, step, oi, slot):
        return remote(
            packed.at[d, step, oi], landed.at[d, step, slot],
            f_send.at[d, step, oi], f_recv.at[d, step, slot], OFFSETS[oi],
        )

    def edge_copy(d, step, side, slot):
        return remote(
            edge_out.at[d, step, side], edge_in.at[d, step, slot],
            e_send.at[d, step, side], e_recv.at[d, step, slot], 1 if side else -1,
        )

    barrier = pltpu.get_barrier_semaphore()
    for offset in OFFSETS:
        @pl.when(present(offset))
        def _():
            pl.semaphore_signal(
                barrier, inc=1, device_id={"tiles": me + offset},
                device_id_type=pl.DeviceIdType.MESH,
            )

    mine[...] = jnp.zeros(mine.shape, jnp.int32)
    for step in range(frame_count - 1):
        mine[step:step + 1, 0:bc] = mf_ref[step:step + 1, :]
        back = frame_count - 2 - step
        mine[frame_count - 1 + step:frame_count + step, 0:bc] = mb_ref[back:back + 1, :]

    identity = (
        lax.broadcasted_iota(jnp.int32, (channels, channels), 0)
        == lax.broadcasted_iota(jnp.int32, (channels, channels), 1)
    ).astype(jnp.bfloat16)
    for d in range(2):
        joined = join_ref[d]
        wj_ref[d, :, :lanes] = blockdiag(joined[:, :channels])
        wj_ref[d, :, lanes:] = blockdiag(joined[:, channels:])


    def build_weights(d):
        def build_layer(layer, carry):
            stacked = conv_ref[d, layer].reshape(9 * channels, channels)
            turned = matmul_t(identity, stacked).astype(jnp.bfloat16)
            blank = jnp.zeros((channels, channels), jnp.bfloat16)

            def tap(down, across):
                start = (3 * down + across) * channels
                return turned[:, start:start + channels]

            for side in range(2):
                order = (0, 1, 2, None) if side == 0 else (1, 0, None, 2)
                depth = (0, 1, 2, None) if side == 0 else (0, 1, None, 2)
                for k, down in enumerate(depth):
                    wc_ref[d, layer, side, k * channels:(k + 1) * channels, :] = jnp.concatenate(
                        [
                            blank if down is None or across is None else tap(down, across)
                            for across in order
                        ],
                        axis=1,
                    )
            return carry

        lax.fori_loop(0, layers, build_layer, 0)

    def picker(count):
        row = lax.broadcasted_iota(jnp.int32, (count, 2 * count), 0)
        column = lax.broadcasted_iota(jnp.int32, (count, 2 * count), 1)
        return ((column == row) | (column == row + count)).astype(jnp.bfloat16)

    def load_frame(f, carry):
        flip[0] = frames_ref[f].astype(jnp.float32).reshape(channels * rows, cols)
        first = lax.broadcasted_iota(jnp.int32, (channels, cols), 1) < width
        parts = []
        for r in range(rows):
            row = flip[0, pl.ds(r, channels, stride=rows), :]
            parts += [jnp.where(first, row, 0.0), jnp.where(first, 0.0, row)]
        moved = matmul_t(picker(width), jnp.concatenate(parts, axis=0).astype(jnp.bfloat16))
        for r in range(rows):
            x_ref[f, r * width:(r + 1) * width, :] = moved[:, r * lanes:(r + 1) * lanes].astype(
                jnp.bfloat16
            )
        return carry

    load_frame(0, 0)
    load_frame(frame_count - 1, 0)

    def emit(d, t):
        value = h_ref[d, halo:halo + own, :].astype(jnp.float32).reshape(rows, width, lanes)
        first = lax.broadcasted_iota(jnp.int32, value.shape, 2) < channels
        split = jnp.concatenate(
            [jnp.where(first, value, 0.0), jnp.where(first, 0.0, value)], axis=1
        ).reshape(rows * cols, lanes).astype(jnp.bfloat16)
        moved = matmul_t(picker(channels), split)
        for r in range(rows):
            flip[d, pl.ds(r, channels, stride=rows), :] = moved[:, r * cols:(r + 1) * cols]
        now = t if d == 0 else frame_count - 1 - t
        outs[d][now] = flip[d].reshape(channels, rows, cols).astype(jnp.bfloat16)

    peers = jnp.minimum(me, REACH) + jnp.minimum(devices - 1 - me, REACH)
    pl.semaphore_wait(barrier, peers)

    for oi, offset in enumerate(OFFSETS):
        @pl.when(present(offset))
        def _():
            motion_copy(oi, sides - 1 - oi).start()

    lane = lax.broadcasted_iota(jnp.int32, mine.shape, 1)

    def prefix(flags):
        total = flags
        shift = 1
        while shift < bc:
            total = total + jnp.where(lane >= shift, pltpu.roll(total, shift, axis=1), 0)
            shift *= 2
        return total - flags

    def owned(motion, device):
        low = device * bc
        return (motion >= low) & (motion < low + bc) & (lane < bc)

    def own_code(local):
        return jnp.where(local < pairs, local, kept + local - pairs)

    def swapped(code):
        return jnp.where(code >= kept, code - kept, code + kept)

    def build_tables():
        motion = mine[...]
        picks = jnp.where(owned(motion, me), own_code(motion - me * bc), 0)
        for oi, offset in enumerate(OFFSETS):
            match = owned(motion, me + offset)
            rank = jnp.minimum(prefix(match.astype(jnp.int32)), cap - 1)
            base = pairs + oi * cap // 2
            code = jnp.where(rank < cap // 2, base + rank, kept + base + rank - cap // 2)
            picks = picks + jnp.where(match, code, 0)
        table_v[sides] = jnp.where(lane < pairs, picks, swapped(picks))
        for oi, offset in enumerate(OFFSETS):
            @pl.when(present(offset))
            def _():
                motion_copy(oi, oi).wait_send()
                motion_copy(oi, oi).wait_recv()
                wanted = theirs[oi]
                match = owned(wanted, me)
                rank = prefix(match.astype(jnp.int32))
                code = own_code(wanted - me * bc)
                gathered = jnp.zeros(mine.shape, jnp.int32)
                for slot in range(cap):
                    held = code if slot < cap // 2 else swapped(code)
                    value = jnp.where(match & (rank == slot), held, 0)
                    shift = 1
                    while shift < bc:
                        value = value + pltpu.roll(value, shift, axis=1)
                        shift *= 2
                    value = pltpu.roll(value, 1 + slot, axis=1)
                    gathered = jnp.where(lane == bc + slot, value, gathered)
                table_v[oi] = gathered

            @pl.when(jnp.logical_not(present(offset)))
            def _():
                table_v[oi] = jnp.zeros(mine.shape, jnp.int32)
        load = pltpu.make_async_copy(table_v, table_s, t_sem)
        load.start()
        load.wait()

    left_half = lax.broadcasted_iota(jnp.int32, (rows, BS, lanes), 2) < channels

    def keep(d, index, tile):
        cand[d, index] = tile
        cand[d, kept + index] = pltpu.roll(tile, channels, axis=2)

    def activate(d, slot, start, value):
        size = value.shape[0]
        z_ref[d, slot, 0, start:start + size, :] = value.astype(jnp.bfloat16)
        z_ref[d, slot, 1, start:start + size, :] = pltpu.roll(value, channels, axis=1).astype(
            jnp.bfloat16
        )

    def begin(d, t):
        @pl.when(t == 0)
        def _():
            aligned[d] = jnp.zeros(aligned.shape[1:], aligned.dtype)

        @pl.when(t > 0)
        def _():
            step = t - 1
            row = d * (frame_count - 1) + step
            for oi, offset in enumerate(OFFSETS):
                @pl.when(present(offset))
                def _():
                    feature_copy(d, step, oi, oi).wait_recv()
                    tiles = landed[d, step, oi].astype(jnp.float32)
                    tiles = tiles.reshape(cap // 2, BS, BS, lanes)
                    for pair in range(cap // 2):
                        keep(d, pairs + oi * cap // 2 + pair, tiles[pair])
            for j in range(pairs):
                low = table_s[sides, row, j]
                high = table_s[sides, row, pairs + j]
                aligned[d, :, j * BS:(j + 1) * BS, :] = jnp.where(
                    left_half, cand[d, low], cand[d, high]
                )

        now = t if d == 0 else frame_count - 1 - t
        both = jnp.concatenate(
            [aligned[d].reshape(own, lanes).astype(jnp.bfloat16), x_ref[now]], axis=1
        )
        first = matmul_t(both, wj_ref[d]).astype(jnp.bfloat16)
        edge_out[d, t, 0] = first[:halo]
        edge_out[d, t, 1] = first[own - halo:]
        for side in range(2):
            @pl.when(present(1 if side else -1))
            def _():
                edge_copy(d, t, side, 1 - side).start()
        h_ref[d, halo:halo + own, :] = first
        activate(d, 0, halo, leaky(first.astype(jnp.float32)))

    top_inside = (me > 0).astype(jnp.float32)
    bottom_inside = (me < devices - 1).astype(jnp.float32)

    def finish(d, t):
        for side in range(2):
            start = side * (halo + own)

            @pl.when(present(1 if side else -1))
            def _():
                edge_copy(d, t, side, side).wait_recv()
                edge = edge_in[d, t, side]
                h_ref[d, start:start + halo, :] = edge
                activate(d, 0, start, leaky(edge.astype(jnp.float32)))

            @pl.when(jnp.logical_not(present(1 if side else -1)))
            def _():
                h_ref[d, start:start + halo, :] = jnp.zeros((halo, lanes), jnp.bfloat16)
                for swap in range(2):
                    z_ref[d, 0, swap, start:start + halo, :] = jnp.zeros(
                        (halo, lanes), jnp.bfloat16
                    )

        for layer in range(layers):
            out_rows = rows + 2 * (layers - 1 - layer)
            size = out_rows * width
            plain = z_ref.at[d, layer % 2, 0]
            turned = z_ref.at[d, layer % 2, 1]
            rows0 = pl.ds(layer * width, size)
            rows1 = pl.ds((layer + 1) * width, size)
            below = plain[(layer + 2) * width:(layer + 2) * width + size, :]
            low = lax.broadcasted_iota(jnp.int32, (size, lanes), 1) < channels
            upper = jnp.where(low, plain[rows0, :], turned[rows1, :])
            lower = jnp.where(low, turned[rows0, :], plain[rows1, :])
            one = jnp.dot(
                jnp.concatenate([upper, below], axis=1), wc_ref[d, layer, 0],
                preferred_element_type=jnp.float32,
            )
            two = jnp.dot(
                jnp.concatenate([lower, below], axis=1), wc_ref[d, layer, 1],
                preferred_element_type=jnp.float32,
            )
            tap0 = jnp.where(low, one[:, :lanes], two[:, :lanes])
            tap1 = pltpu.roll(jnp.where(low, two[:, :lanes], one[:, :lanes]), channels, axis=1)
            tap2 = jnp.where(low, one[:, lanes:], two[:, lanes:])
            place = lax.broadcasted_iota(jnp.int32, (out_rows, BS, lanes), 1)
            lefts = lax.broadcasted_iota(jnp.int32, (out_rows, BS, lanes), 2) < channels
            before = pltpu.roll(tap0.reshape(out_rows, width, lanes), 1, axis=1)
            seam = before[:, :BS]
            crossed = jnp.where(lefts, 0.0, pltpu.roll(seam, channels, axis=2))
            before = jnp.concatenate(
                [jnp.where(place == 0, crossed, seam), before[:, BS:]], axis=1
            ).reshape(size, lanes)
            after = pltpu.roll(tap2.reshape(out_rows, width, lanes), width - 1, axis=1)
            seam = after[:, width - BS:]
            crossed = jnp.where(lefts, pltpu.roll(seam, channels, axis=2), 0.0)
            after = jnp.concatenate(
                [after[:, :width - BS], jnp.where(place == BS - 1, crossed, seam)], axis=1
            ).reshape(size, lanes)
            base = (layer + 1) * width
            total = h_ref[d, base:base + size, :].astype(jnp.float32) + tap1
            rounded = (total + before + after).astype(jnp.bfloat16)
            if layer < layers - 1:
                h_ref[d, base:base + size, :] = rounded
                active = leaky(rounded.astype(jnp.float32))
                outside = halo - base
                active = jnp.concatenate(
                    [
                        active[:outside] * top_inside,
                        active[outside:size - outside],
                        active[size - outside:] * bottom_inside,
                    ],
                    axis=0,
                )
                activate(d, 1 - layer % 2, base, active)
            else:
                grid = rounded.astype(jnp.float32).reshape(rows, pairs, BS, lanes)
                for j in range(pairs):
                    keep(d, j, grid[:, j])
                h_ref[d, base:base + size, :] = rounded

        @pl.when(t < frame_count - 1)
        def _():
            row = d * (frame_count - 1) + t
            for oi, offset in enumerate(OFFSETS):
                @pl.when(present(offset))
                def _():
                    for pair in range(cap // 2):
                        low = table_s[oi, row, bc + pair]
                        high = table_s[oi, row, bc + cap // 2 + pair]
                        block = jnp.where(left_half, cand[d, low], cand[d, high])
                        packed[d, t, oi, pair * cell:(pair + 1) * cell, :] = block.reshape(
                            cell, lanes
                        ).astype(jnp.bfloat16)
                    feature_copy(d, t, oi, sides - 1 - oi).start()

    def frame_step(t, carry):
        begin(0, t)
        begin(1, t)

        @pl.when(t == 0)
        def _():
            build_weights(0)
            build_weights(1)
            lax.fori_loop(1, frame_count - 1, load_frame, 0)
            build_tables()

        finish(0, t)
        finish(1, t)
        emit(0, t)
        emit(1, t)
        return carry

    lax.fori_loop(0, frame_count, frame_step, 0)

    for d in range(2):
        for step in range(frame_count):
            for side in range(2):
                @pl.when(present(1 if side else -1))
                def _():
                    edge_copy(d, step, side, side).wait_send()
            if step < frame_count - 1:
                for oi, offset in enumerate(OFFSETS):
                    @pl.when(present(offset))
                    def _():
                        feature_copy(d, step, oi, oi).wait_send()


def on_device(frames, motion_forward, motion_backward, join_weight, conv_weight):
    frame_count, channels, rows, cols = frames.shape
    layers = conv_weight.shape[1]
    devices = lax.axis_size("tiles")
    lanes = 2 * channels
    width = cols // 2
    own = rows * width
    halo = layers * width
    bc = rows // BS * (cols // BS)
    cap = bc // (2 * REACH)
    sides = len(OFFSETS)
    steps = frame_count - 1
    kept = bc // 2 + sides * cap // 2

    dims = (frame_count, rows, cols, channels, layers, devices)
    vmem = pl.BlockSpec(memory_space=pltpu.VMEM)
    result = jax.ShapeDtypeStruct(frames.shape, jnp.bfloat16)
    return pl.pallas_call(
        functools.partial(sweep_kernel, dims),
        out_shape=(result, result),
        in_specs=[vmem] * 5,
        out_specs=(vmem, vmem),
        scratch_shapes=[
            pltpu.VMEM((frame_count, own, lanes), jnp.bfloat16),
            pltpu.VMEM((2, channels * rows, cols), jnp.float32),
            pltpu.VMEM((2, lanes, 2 * lanes), jnp.bfloat16),
            pltpu.VMEM((2, layers, 2, 2 * lanes, 2 * lanes), jnp.bfloat16),
            pltpu.VMEM((8, 128), jnp.int32),
            pltpu.VMEM((sides, 8, 128), jnp.int32),
            pltpu.VMEM((sides + 1, 8, 128), jnp.int32),
            pltpu.SMEM((sides + 1, 8, 128), jnp.int32),
            pltpu.VMEM((2, 2 * kept, BS, BS, lanes), jnp.float32),
            pltpu.VMEM((2, steps, sides, cap // 2 * BS * BS, lanes), jnp.bfloat16),
            pltpu.VMEM((2, steps, sides, cap // 2 * BS * BS, lanes), jnp.bfloat16),
            pltpu.VMEM((2, rows, width, lanes), jnp.float32),
            pltpu.VMEM((2, own + 2 * halo, lanes), jnp.bfloat16),
            pltpu.VMEM((2, 2, 2, own + 2 * halo, lanes), jnp.bfloat16),
            pltpu.VMEM((2, frame_count, 2, halo, lanes), jnp.bfloat16),
            pltpu.VMEM((2, frame_count, 2, halo, lanes), jnp.bfloat16),
            pltpu.SemaphoreType.DMA((sides,)),
            pltpu.SemaphoreType.DMA((sides,)),
            pltpu.SemaphoreType.DMA((2, steps, sides)),
            pltpu.SemaphoreType.DMA((2, steps, sides)),
            pltpu.SemaphoreType.DMA((2, frame_count, 2)),
            pltpu.SemaphoreType.DMA((2, frame_count, 2)),
            pltpu.SemaphoreType.DMA,
        ],
        compiler_params=pltpu.CompilerParams(
            collective_id=0, has_side_effects=True, vmem_limit_bytes=56 * 1024 * 1024
        ),
    )(frames, motion_forward, motion_backward, join_weight, conv_weight)


def solution(mesh):
    return jax.shard_map(
        on_device,
        mesh=mesh,
        in_specs=(
            P(None, None, ("clips", "tiles"), None),
            P(None, ("clips", "tiles")),
            P(None, ("clips", "tiles")),
            P(),
            P(),
        ),
        out_specs=(
            P(None, None, ("clips", "tiles"), None),
            P(None, None, ("clips", "tiles"), None),
        ),
        check_vma=False,
    )
```
